32 devices in a mesh: dp: 8 (over y, x, core), ctx: 4 (over z).
Axes of the slice: x: 2, y: 2, z: 4, core: 2. Of those that a mesh axis runs over, the one named last changes fastest.
Arguments:
- queries: bfloat16 [8192, 2048], P(('dp', 'ctx')), parts along dimension 0, may hold values from -18 to 18
- key_vectors: bfloat16 [8192, 2048], P(('dp', 'ctx')), parts along dimension 0, may hold values from -18 to 18
- value_vectors: bfloat16 [8192, 2048], P(('dp', 'ctx')), parts along dimension 0, may hold values from -6 to 6
- norm_gain: float32 [2048], replicated, may hold values from 0.1 to 1.9
- window_gain: float32 [2048], replicated, may hold values from 0.1 to 1.9
Outputs:
- mixed: bfloat16 [8192, 2048], P(('dp', 'ctx')), parts along dimension 0
The draws below stay inside these ranges and needn't reach their ends.
There are 8 independent parts, one for each index of `dp`. The reference program is written for one: setup_inputs(seed, part) draws one part's arguments, and reference() takes and returns one part's arrays. A program takes and returns all parts, laid end to end along the dimension named above; an argument that names none is the same for every part. Nothing has to cross between parts.
All inputs are finite; a program needn't handle non-finite values.
Results may differ from the reference program's by a relative error of at most 0.0037.
Values may be sent and summed in bfloat16 or wider, within the bound.
A program may use at most 128 MiB of HBM per device.

```python
import math
import jax
import jax.numpy as jnp
from jax import lax

HEADS = 16
HEAD = 128
D = 2048
WINDOW = 1024
TOK_DEV = 256
SEQ = 1024


def draw_queries(key, part):
    drawn = jnp.clip(jax.random.normal(jax.random.fold_in(key, 1), (SEQ, D), jnp.float32), -6.0, 6.0)
    return drawn.astype(jnp.bfloat16)


def draw_key_vectors(key, part):
    drawn = jnp.clip(jax.random.normal(jax.random.fold_in(key, 3), (SEQ, D), jnp.float32), -6.0, 6.0)
    return drawn.astype(jnp.bfloat16)


def level_of(own_key, extent, cuts, least, top_value):
    def one(position, parts):
        draws = jax.random.uniform(jax.random.fold_in(jax.random.fold_in(own_key, 6), position), (parts,), jnp.float32, least / len(cuts), top_value / len(cuts))
        return jnp.repeat(jnp.exp(draws), extent[position] // parts).reshape((-1,) + (1,) * (len(extent) - position - 1))

    level = one(*cuts[0])
    for cut in cuts[1:]:
        level = level * one(*cut)
    return level


def noise(rng, dims, deviation, most, shards=(), kind=jnp.bfloat16):
    entries = jax.random.normal(rng, dims, jnp.float32) * deviation
    if len(shards) > 0:
        entries = level_of(rng, dims, shards, -0.22, 0.18) * entries
    return jnp.clip(entries, min=-most, max=most).astype(kind)


def setup_inputs(seed: int = 0, part: int = 0) -> dict:
    splits = jax.random.split(jax.random.key(seed), 6)
    own_keys = jax.random.split(jax.random.fold_in(splits[5], part), 6)
    queries = draw_queries(jax.random.fold_in(jax.random.fold_in(splits[5], part), 71), part)
    key_vectors = draw_key_vectors(jax.random.fold_in(jax.random.fold_in(splits[5], part), 71), part)
    value_vectors = noise(own_keys[2], (SEQ, D), 1.0, 6.0, ((0, 4),))
    norm_gain = jnp.clip(1.0 + 0.18 * jax.random.normal(splits[3], (D,), jnp.float32), 0.1, 1.9)
    window_gain = jnp.clip(1.0 + 0.18 * jax.random.normal(splits[4], (D,), jnp.float32), 0.1, 1.9)
    return dict(queries=queries, key_vectors=key_vectors, value_vectors=value_vectors, norm_gain=norm_gain, window_gain=window_gain)


def feature_map(values):
    upcast = values.astype(jnp.float32)
    return jnp.where(upcast > 0, upcast + 1.0, jnp.exp(jnp.minimum(upcast, 0.0))).astype(jnp.bfloat16)

def reference(queries, key_vectors, value_vectors, norm_gain, window_gain):
    length = queries.shape[0]
    query_heads = queries.reshape(length, HEADS, HEAD).transpose(1, 0, 2)
    key_heads = key_vectors.reshape(length, HEADS, HEAD).transpose(1, 0, 2)
    value_heads = value_vectors.reshape(length, HEADS, HEAD).transpose(1, 0, 2)
    positions = jnp.arange(length)
    inside = (positions[:, None] >= positions[None, :]) & (positions[:, None] - positions[None, :] < WINDOW)
    scale = 1.0 / math.sqrt(HEAD)

    def attend(operands):
        query_head, key_head, value_head = operands
        scores = jnp.dot(query_head, key_head.T, preferred_element_type=jnp.float32) * scale
        scores = jnp.where(inside, scores, -jnp.inf)
        peak = lax.optimization_barrier(jnp.max(scores, axis=-1, keepdims=True))
        expos = jnp.exp(scores - peak)
        weights = (expos / lax.optimization_barrier(jnp.sum(expos, axis=-1, keepdims=True))).astype(jnp.bfloat16)
        return jnp.dot(weights, value_head, preferred_element_type=jnp.float32)
    attended = lax.map(attend, (query_heads, key_heads, value_heads)).transpose(1, 0, 2)
    windowed = attended * lax.rsqrt(lax.optimization_barrier(jnp.mean(attended * attended, axis=-1, keepdims=True)) + 1e-05)
    windowed = windowed * window_gain.astype(jnp.float32).reshape(HEADS, HEAD)
    blocks = length // TOK_DEV
    phi_query = feature_map(queries).reshape(blocks, TOK_DEV, HEADS, HEAD).astype(jnp.float32)
    phi_key = feature_map(key_vectors).reshape(blocks, TOK_DEV, HEADS, HEAD).astype(jnp.float32)
    value_blocks = value_vectors.reshape(blocks, TOK_DEV, HEADS, HEAD).astype(jnp.float32)
    block_state = jnp.einsum('cthe,cthf->chef', phi_key, value_blocks)
    shifted = jnp.concatenate([jnp.zeros_like(block_state[:1]), block_state[:-1]], axis=0)
    carried = jnp.cumsum(shifted, axis=0).astype(jnp.bfloat16).astype(jnp.float32)
    from_state = jnp.einsum('cthe,chef->cthf', phi_query, carried)
    affinity = jnp.einsum('cthe,cshe->chts', phi_query, phi_key)
    inner = jnp.arange(TOK_DEV)
    causal = inner[:, None] >= inner[None, :]
    affinity = jnp.where(causal, affinity, 0.0).astype(jnp.bfloat16).astype(jnp.float32)
    local_part = jnp.einsum('chts,cshf->cthf', affinity, value_blocks)
    linear = (from_state + local_part).reshape(length, HEADS, HEAD)
    normed = linear * lax.rsqrt(lax.optimization_barrier(jnp.mean(linear * linear, axis=-1, keepdims=True)) + 1e-05)
    normed = normed * norm_gain.astype(jnp.float32).reshape(HEADS, HEAD)
    return (windowed + normed).reshape(length, HEADS * HEAD).astype(jnp.bfloat16)
```

```python
import functools
import math

import jax
import jax.numpy as jnp
from jax import lax
from jax.experimental import pallas as pl
from jax.experimental.pallas import tpu as pltpu
from jax.sharding import PartitionSpec as P

HEAD = 128
WINDOW = 1024
EPS = 1e-05


def passed_along(value, axis, steps):
    count = lax.axis_size(axis)
    leading, last = (max(0, -steps), min(count, count - steps))
    return lax.ppermute(value, axis, [(source, source + steps) for source in range(leading, last)])


def entering(array, axis, combine, identity):
    peers, position = (lax.axis_size(axis), lax.axis_index(axis))
    everything = lax.all_gather(array.astype(jnp.bfloat16), axis)
    start = jnp.broadcast_to(jnp.asarray(identity, array.dtype), array.shape)

    def lap(k, before):
        reached = k < position
        new = combine(before, everything[k].astype(array.dtype))
        return jnp.where(reached, new, before)

    return lax.fori_loop(0, peers, lap, start)


def feature_map(values):
    upcast = values.astype(jnp.float32)
    return jnp.where(upcast > 0, upcast + 1.0, jnp.exp(jnp.minimum(upcast, 0.0))).astype(
        jnp.bfloat16
    )


def add_states(earlier, later):
    return earlier + later


def shards(queries, key_vectors, value_vectors, norm_gain, window_gain):
    tok_rows, model_width = queries.shape
    head_count = model_width // HEAD
    ctx_index = lax.axis_index("ctx")
    reach_blocks = WINDOW // tok_rows
    own_pair = (key_vectors, value_vectors)
    received = []
    travelling = own_pair
    for distance in range(reach_blocks):
        travelling = passed_along((travelling[0], travelling[1]), "ctx", 1)
        received.append(travelling)
    ordered = received[::-1] + [own_pair]
    window_keys = jnp.concatenate([member[0] for member in ordered], axis=0)
    window_values = jnp.concatenate([member[1] for member in ordered], axis=0)
    span_rows = window_keys.shape[0]
    query_place = ctx_index * tok_rows + jnp.arange(tok_rows, dtype=jnp.int32)
    key_place = (ctx_index - reach_blocks) * tok_rows + jnp.arange(span_rows, dtype=jnp.int32)
    inside = (
        (key_place[None, :] <= query_place[:, None])
        & (query_place[:, None] - key_place[None, :] < WINDOW)
        & (key_place[None, :] >= 0)
    )
    group_size = 4
    groups = head_count // group_size
    scale = 1.0 / math.sqrt(HEAD)

    def split_groups(matrix):
        return jnp.moveaxis(matrix.reshape(matrix.shape[0], groups, group_size, HEAD), 1, 0)

    def attend(operands):
        query_group, key_group, value_group = operands
        scores = (
            jnp.einsum("tge,sge->gts", query_group, key_group, preferred_element_type=jnp.float32)
            * scale
        )
        scores = jnp.where(inside[None], scores, -jnp.inf)
        peak = jnp.max(scores, axis=-1, keepdims=True)
        expos = jnp.exp(scores - peak)
        weights = (expos / jnp.sum(expos, axis=-1, keepdims=True)).astype(jnp.bfloat16)
        return jnp.einsum("gts,sge->tge", weights, value_group, preferred_element_type=jnp.float32)

    attended = lax.map(
        attend, (split_groups(queries), split_groups(window_keys), split_groups(window_values))
    )
    attended = jnp.moveaxis(attended, 0, 1).reshape(tok_rows, head_count, HEAD)
    windowed = attended * lax.rsqrt(jnp.mean(attended * attended, axis=-1, keepdims=True) + EPS)
    windowed = windowed * window_gain.reshape(head_count, HEAD)
    phi_query = feature_map(queries).reshape(tok_rows, head_count, HEAD)
    phi_key = feature_map(key_vectors).reshape(tok_rows, head_count, HEAD)
    value_heads = value_vectors.reshape(tok_rows, head_count, HEAD)
    local_state = jnp.einsum(
        "the,thf->hef", phi_key, value_heads, preferred_element_type=jnp.float32
    )
    carried = entering(local_state, "ctx", add_states, jnp.zeros_like(local_state))
    from_state = jnp.einsum(
        "the,hef->thf", phi_query, carried.astype(jnp.bfloat16), preferred_element_type=jnp.float32
    )
    affinity = jnp.einsum("the,she->hts", phi_query, phi_key, preferred_element_type=jnp.float32)
    inner = jnp.arange(tok_rows, dtype=jnp.int32)
    causal = inner[:, None] >= inner[None, :]
    affinity = jnp.where(causal[None], affinity, 0.0).astype(jnp.bfloat16)
    local_part = jnp.einsum(
        "hts,shf->thf", affinity, value_heads, preferred_element_type=jnp.float32
    )
    linear = from_state + local_part
    normed = linear * lax.rsqrt(jnp.mean(linear * linear, axis=-1, keepdims=True) + EPS)
    normed = normed * norm_gain.reshape(head_count, HEAD)
    return (windowed + normed).reshape(tok_rows, model_width).astype(jnp.bfloat16)


QA, QB, KK, VV, OA, OB, ST, SN = range(8)
EXP_SCALE = math.log2(math.e) / math.sqrt(HEAD)
LOW = -1e30


def nt(a, b):
    return lax.dot_general(a, b, (((1,), (1,)), ((), ())), preferred_element_type=jnp.float32)


def tn(a, b):
    return lax.dot_general(a, b, (((0,), (0,)), ((), ())), preferred_element_type=jnp.float32)


def tt(a, b):
    return lax.dot_general(a, b, (((0,), (1,)), ((), ())), preferred_element_type=jnp.float32)


def hub_kernel(
    n,
    q_ref, k_ref, v_ref, gn_ref, gw_ref, out_ref,
    qa, qb, kr, vr, oa_s, ob_s, st_s, sn_s, oa_r, ob_r, st_r, sn_r,
    send, recv,
):
    tok, width = q_ref.shape
    heads = width // HEAD
    me = lax.axis_index("ctx")
    left, right = me - 1, me + 1
    first, hub, last = 0, 1, n - 1

    def cols(h):
        return pl.ds(pl.multiple_of(h * HEAD, HEAD), HEAD)

    def move(stream, src, dst, h, target):
        return pltpu.make_async_remote_copy(
            src_ref=src,
            dst_ref=dst,
            send_sem=send.at[stream, h],
            recv_sem=recv.at[stream, h],
            device_id={"ctx": target},
            device_id_type=pl.DeviceIdType.MESH,
        )

    def q_left(h):
        return move(QA, q_ref.at[:, cols(h)], qa.at[:, cols(h)], h, left)

    def q_relay(h):
        return move(QB, qa.at[:, cols(h)], qb.at[:, cols(h)], h, left)

    def k_right(h):
        return move(KK, k_ref.at[:, cols(h)], kr.at[:, cols(h)], h, right)

    def v_right(h):
        return move(VV, v_ref.at[:, cols(h)], vr.at[:, cols(h)], h, right)

    def oa_right(h):
        return move(OA, oa_s.at[h], oa_r.at[h], h, right)

    def ob_right(h):
        return move(OB, ob_s.at[h], ob_r.at[h], h, right)

    def st_right(h):
        return move(ST, st_s.at[h], st_r.at[h], h, right)

    def sn_right(h):
        return move(SN, sn_s.at[h], sn_r.at[h], h, right)

    def each_head(body):
        def step(h, carry):
            body(h)
            return carry

        lax.fori_loop(0, heads, step, 0)

    barrier = pltpu.get_barrier_semaphore()

    @pl.when(me > first)
    def _():
        pl.semaphore_signal(
            barrier, inc=1, device_id={"ctx": left}, device_id_type=pl.DeviceIdType.MESH
        )

    @pl.when(me < last)
    def _():
        pl.semaphore_signal(
            barrier, inc=1, device_id={"ctx": right}, device_id_type=pl.DeviceIdType.MESH
        )

    peers = (me > first).astype(jnp.int32) + (me < last).astype(jnp.int32)
    pl.semaphore_wait(barrier, peers)

    key_at = lax.broadcasted_iota(jnp.int32, (tok, tok), 0)
    query_at = lax.broadcasted_iota(jnp.int32, (tok, tok), 1)
    causal = key_at <= query_at

    def soft(scores, values):
        peak = functools.reduce(
            jnp.maximum, [jnp.max(s, axis=0, keepdims=True) for s in scores]
        )
        total, out = 0.0, 0.0
        for s, v in zip(scores, values):
            e = jnp.exp2((s - peak) * EXP_SCALE)
            total = total + jnp.sum(e, axis=0, keepdims=True)
            out = out + tn(v, e.astype(jnp.bfloat16))
        return peak, total, out

    def merge(one, peak, total, out):
        top = jnp.maximum(one[0], peak)
        f1 = jnp.exp2((one[0] - top) * EXP_SCALE)
        f2 = jnp.exp2((peak - top) * EXP_SCALE)
        return top, one[1] * f1 + total * f2, one[2] * f1 + out.astype(jnp.float32) * f2

    def local_linear(q, phi_k, v):
        phi_q = feature_map(q)
        affinity = jnp.where(causal, nt(phi_k, phi_q), 0.0).astype(jnp.bfloat16)
        return phi_q, tn(v, affinity)

    def finish(h, soft_sum, linear):
        _, total, out = soft_sum
        att = out * (1.0 / total)
        att = att * lax.rsqrt(jnp.mean(att * att, axis=0, keepdims=True) + EPS)
        lin = linear * lax.rsqrt(jnp.mean(linear * linear, axis=0, keepdims=True) + EPS)
        row = att.T * gw_ref[pl.ds(h, 1), :] + lin.T * gn_ref[pl.ds(h, 1), :]
        out_ref[:, cols(h)] = row.astype(jnp.bfloat16)

    def diagonal(q, k):
        return jnp.where(causal, nt(k, q), LOW)

    @pl.when(me == first)
    def _():
        def start(h):
            k_right(h).start()
            v_right(h).start()

        each_head(start)

        def compute(h):
            q, k, v = q_ref[:, cols(h)], k_ref[:, cols(h)], v_ref[:, cols(h)]
            _, linear = local_linear(q, feature_map(k), v)
            finish(h, soft([diagonal(q, k)], [v]), linear)

        each_head(compute)

        def drain(h):
            k_right(h).wait_send()
            v_right(h).wait_send()

        each_head(drain)

    @pl.when(me == hub)
    def _():
        def compute(h):
            k_right(h).wait_recv()
            v_right(h).wait_recv()
            q_left(h).wait_recv()
            q_relay(h).wait_recv()
            q, k, v = q_ref[:, cols(h)], k_ref[:, cols(h)], v_ref[:, cols(h)]
            k0, v0 = kr[:, cols(h)], vr[:, cols(h)]
            q2, q3 = qa[:, cols(h)], qb[:, cols(h)]
            peak, total, out = soft([nt(k0, q3), nt(k, q3)], [v0, v])
            ob_s[h] = out.astype(jnp.bfloat16)
            st_s[h, 2:3] = peak
            st_s[h, 3:4] = total
            peak, total, out = soft([nt(k0, q2), nt(k, q2)], [v0, v])
            oa_s[h] = out.astype(jnp.bfloat16)
            st_s[h, 0:1] = peak
            st_s[h, 1:2] = total
            phi_k = feature_map(k)
            before = tn(feature_map(k0), v0)
            sn_s[h] = (before + tn(phi_k, v)).astype(jnp.bfloat16)
            st_right(h).start()
            ob_right(h).start()
            sn_right(h).start()
            oa_right(h).start()
            phi_q, linear = local_linear(q, phi_k, v)
            linear = linear + tt(before.astype(jnp.bfloat16), phi_q)
            finish(h, soft([nt(k0, q), diagonal(q, k)], [v0, v]), linear)

        each_head(compute)

        def drain(h):
            st_right(h).wait_send()
            ob_right(h).wait_send()
            sn_right(h).wait_send()
            oa_right(h).wait_send()

        each_head(drain)

    @pl.when((me > hub) & (me < last))
    def _():
        def relay(h):
            q_left(h).start()
            q_left(h).wait_recv()
            q_relay(h).start()

        each_head(relay)

        def compute(h):
            q, k, v = q_ref[:, cols(h)], k_ref[:, cols(h)], v_ref[:, cols(h)]
            phi_k = feature_map(k)
            phi_q, linear = local_linear(q, phi_k, v)
            state = tn(phi_k, v)
            other = soft([nt(k, qa[:, cols(h)])], [v])
            own = soft([diagonal(q, k)], [v])
            st_right(h).wait_recv()
            ob_right(h).wait_recv()
            stats = st_r[h]
            peak, total, out = merge(other, stats[2:3], stats[3:4], ob_r[h])
            oa_s[h] = out.astype(jnp.bfloat16)
            st_s[h, 0:1] = peak
            st_s[h, 1:2] = total
            st_s[h, 2:3] = peak
            st_s[h, 3:4] = total
            st_right(h).start()
            oa_right(h).start()
            sn_right(h).wait_recv()
            carried = sn_r[h]
            sn_s[h] = (carried.astype(jnp.float32) + state).astype(jnp.bfloat16)
            sn_right(h).start()
            linear = linear + tt(carried, phi_q)
            oa_right(h).wait_recv()
            finish(h, merge(own, stats[0:1], stats[1:2], oa_r[h]), linear)

        each_head(compute)

        def drain(h):
            q_left(h).wait_send()
            q_relay(h).wait_send()
            st_right(h).wait_send()
            oa_right(h).wait_send()
            sn_right(h).wait_send()

        each_head(drain)

    @pl.when(me == last)
    def _():
        def start(h):
            q_left(h).start()

        each_head(start)

        def compute(h):
            q, k, v = q_ref[:, cols(h)], k_ref[:, cols(h)], v_ref[:, cols(h)]
            phi_q, linear = local_linear(q, feature_map(k), v)
            own = soft([diagonal(q, k)], [v])
            st_right(h).wait_recv()
            sn_right(h).wait_recv()
            linear = linear + tt(sn_r[h], phi_q)
            stats = st_r[h]
            oa_right(h).wait_recv()
            finish(h, merge(own, stats[0:1], stats[1:2], oa_r[h]), linear)

        each_head(compute)

        def drain(h):
            q_left(h).wait_send()

        each_head(drain)


def hub_shards(n, queries, key_vectors, value_vectors, norm_gain, window_gain):
    tok, width = queries.shape
    heads = width // HEAD
    vmem = pl.BlockSpec(memory_space=pltpu.VMEM)
    block = pltpu.VMEM((tok, width), jnp.bfloat16)
    partial = pltpu.VMEM((heads, HEAD, tok), jnp.bfloat16)
    stats = pltpu.VMEM((heads, 4, tok), jnp.float32)
    state = pltpu.VMEM((heads, HEAD, HEAD), jnp.bfloat16)
    return pl.pallas_call(
        functools.partial(hub_kernel, n),
        out_shape=jax.ShapeDtypeStruct((tok, width), jnp.bfloat16),
        in_specs=[vmem] * 5,
        out_specs=vmem,
        scratch_shapes=[block] * 4
        + [partial, partial, stats, state] * 2
        + [pltpu.SemaphoreType.DMA((8, heads)), pltpu.SemaphoreType.DMA((8, heads))],
        compiler_params=pltpu.CompilerParams(
            collective_id=0, has_side_effects=True, vmem_limit_bytes=56 * 2**20
        ),
        name="hub_attention",
    )(
        queries,
        key_vectors,
        value_vectors,
        norm_gain.reshape(heads, HEAD),
        window_gain.reshape(heads, HEAD),
    )


def solution(mesh):
    count = mesh.shape["ctx"]

    def run(queries, key_vectors, value_vectors, norm_gain, window_gain):
        args = (queries, key_vectors, value_vectors, norm_gain, window_gain)
        fits = count * queries.shape[0] <= WINDOW
        if fits and count - 2 == 2:
            return hub_shards(count, *args)
        return shards(*args)

    return jax.shard_map(
        run,
        mesh=mesh,
        in_specs=(P(("dp", "ctx"), None), P(("dp", "ctx"), None), P(("dp", "ctx"), None), P(), P()),
        out_specs=P(("dp", "ctx"), None),
        check_vma=False,
    )
```

```python
import functools
import math

import jax
import jax.numpy as jnp
from jax import lax
from jax.experimental import pallas as pl
from jax.experimental.pallas import tpu as pltpu
from jax.sharding import PartitionSpec as P

HEAD = 128
WINDOW = 1024
EPS = 1e-05


def passed_along(value, axis, steps):
    count = lax.axis_size(axis)
    leading, last = (max(0, -steps), min(count, count - steps))
    return lax.ppermute(value, axis, [(source, source + steps) for source in range(leading, last)])


def entering(array, axis, combine, identity):
    peers, position = (lax.axis_size(axis), lax.axis_index(axis))
    everything = lax.all_gather(array.astype(jnp.bfloat16), axis)
    start = jnp.broadcast_to(jnp.asarray(identity, array.dtype), array.shape)

    def lap(k, before):
        reached = k < position
        new = combine(before, everything[k].astype(array.dtype))
        return jnp.where(reached, new, before)

    return lax.fori_loop(0, peers, lap, start)


def feature_map(values):
    upcast = values.astype(jnp.float32)
    return jnp.where(upcast > 0, upcast + 1.0, jnp.exp(jnp.minimum(upcast, 0.0))).astype(
        jnp.bfloat16
    )


def add_states(earlier, later):
    return earlier + later


def shards(queries, key_vectors, value_vectors, norm_gain, window_gain):
    tok_rows, model_width = queries.shape
    head_count = model_width // HEAD
    ctx_index = lax.axis_index("ctx")
    reach_blocks = WINDOW // tok_rows
    own_pair = (key_vectors, value_vectors)
    received = []
    travelling = own_pair
    for distance in range(reach_blocks):
        travelling = passed_along((travelling[0], travelling[1]), "ctx", 1)
        received.append(travelling)
    ordered = received[::-1] + [own_pair]
    window_keys = jnp.concatenate([member[0] for member in ordered], axis=0)
    window_values = jnp.concatenate([member[1] for member in ordered], axis=0)
    span_rows = window_keys.shape[0]
    query_place = ctx_index * tok_rows + jnp.arange(tok_rows, dtype=jnp.int32)
    key_place = (ctx_index - reach_blocks) * tok_rows + jnp.arange(span_rows, dtype=jnp.int32)
    inside = (
        (key_place[None, :] <= query_place[:, None])
        & (query_place[:, None] - key_place[None, :] < WINDOW)
        & (key_place[None, :] >= 0)
    )
    group_size = 4
    groups = head_count // group_size
    scale = 1.0 / math.sqrt(HEAD)

    def split_groups(matrix):
        return jnp.moveaxis(matrix.reshape(matrix.shape[0], groups, group_size, HEAD), 1, 0)

    def attend(operands):
        query_group, key_group, value_group = operands
        scores = (
            jnp.einsum("tge,sge->gts", query_group, key_group, preferred_element_type=jnp.float32)
            * scale
        )
        scores = jnp.where(inside[None], scores, -jnp.inf)
        peak = jnp.max(scores, axis=-1, keepdims=True)
        expos = jnp.exp(scores - peak)
        weights = (expos / jnp.sum(expos, axis=-1, keepdims=True)).astype(jnp.bfloat16)
        return jnp.einsum("gts,sge->tge", weights, value_group, preferred_element_type=jnp.float32)

    attended = lax.map(
        attend, (split_groups(queries), split_groups(window_keys), split_groups(window_values))
    )
    attended = jnp.moveaxis(attended, 0, 1).reshape(tok_rows, head_count, HEAD)
    windowed = attended * lax.rsqrt(jnp.mean(attended * attended, axis=-1, keepdims=True) + EPS)
    windowed = windowed * window_gain.reshape(head_count, HEAD)
    phi_query = feature_map(queries).reshape(tok_rows, head_count, HEAD)
    phi_key = feature_map(key_vectors).reshape(tok_rows, head_count, HEAD)
    value_heads = value_vectors.reshape(tok_rows, head_count, HEAD)
    local_state = jnp.einsum(
        "the,thf->hef", phi_key, value_heads, preferred_element_type=jnp.float32
    )
    carried = entering(local_state, "ctx", add_states, jnp.zeros_like(local_state))
    from_state = jnp.einsum(
        "the,hef->thf", phi_query, carried.astype(jnp.bfloat16), preferred_element_type=jnp.float32
    )
    affinity = jnp.einsum("the,she->hts", phi_query, phi_key, preferred_element_type=jnp.float32)
    inner = jnp.arange(tok_rows, dtype=jnp.int32)
    causal = inner[:, None] >= inner[None, :]
    affinity = jnp.where(causal[None], affinity, 0.0).astype(jnp.bfloat16)
    local_part = jnp.einsum(
        "hts,shf->thf", affinity, value_heads, preferred_element_type=jnp.float32
    )
    linear = from_state + local_part
    normed = linear * lax.rsqrt(jnp.mean(linear * linear, axis=-1, keepdims=True) + EPS)
    normed = normed * norm_gain.reshape(head_count, HEAD)
    return (windowed + normed).reshape(tok_rows, model_width).astype(jnp.bfloat16)


QA, QB, KK, VV, OA, OB, ST, SN = range(8)
EXP_SCALE = math.log2(math.e) / math.sqrt(HEAD)
LOW = -1e30


def nt(a, b):
    return lax.dot_general(a, b, (((1,), (1,)), ((), ())), preferred_element_type=jnp.float32)


def tn(a, b):
    return lax.dot_general(a, b, (((0,), (0,)), ((), ())), preferred_element_type=jnp.float32)


def tt(a, b):
    return lax.dot_general(a, b, (((0,), (1,)), ((), ())), preferred_element_type=jnp.float32)


def hub_kernel(
    n,
    q_ref, k_ref, v_ref, gn_ref, gw_ref, out_ref,
    qa, qb, kr, vr, oa_s, ob_s, st_s, sn_s, oa_r, ob_r, st_r, sn_r,
    q_own, k_own, v_own, mixed, send, recv, loaded, stored,
):
    tok, width = q_ref.shape
    heads = width // HEAD
    me = lax.axis_index("ctx")
    left, right = me - 1, me + 1
    first, hub, last = 0, 1, n - 1

    def cols(h):
        return pl.ds(pl.multiple_of(h * HEAD, HEAD), HEAD)

    def move(stream, src, dst, h, target):
        return pltpu.make_async_remote_copy(
            src_ref=src,
            dst_ref=dst,
            send_sem=send.at[stream, h],
            recv_sem=recv.at[stream, h],
            device_id={"ctx": target},
            device_id_type=pl.DeviceIdType.MESH,
        )

    def q_left(h):
        return move(QA, q_ref.at[:, cols(h)], qa.at[:, cols(h)], h, left)

    def q_relay(h):
        return move(QB, qa.at[:, cols(h)], qb.at[:, cols(h)], h, left)

    def k_right(h):
        return move(KK, k_ref.at[:, cols(h)], kr.at[:, cols(h)], h, right)

    def v_right(h):
        return move(VV, v_ref.at[:, cols(h)], vr.at[:, cols(h)], h, right)

    def oa_right(h):
        return move(OA, oa_s.at[h], oa_r.at[h], h, right)

    def ob_right(h):
        return move(OB, ob_s.at[h], ob_r.at[h], h, right)

    def st_right(h):
        return move(ST, st_s.at[h], st_r.at[h], h, right)

    def sn_right(h):
        return move(SN, sn_s.at[h], sn_r.at[h], h, right)

    def each_head(body):
        def step(h, carry):
            body(h)
            return carry

        lax.fori_loop(0, heads, step, 0)

    loads = [
        pltpu.make_async_copy(src, dst, loaded.at[i])
        for i, (src, dst) in enumerate([(k_ref, k_own), (v_ref, v_own), (q_ref, q_own)])
    ]
    for load in loads:
        load.start()

    def store(h):
        return pltpu.make_async_copy(mixed.at[:, cols(h)], out_ref.at[:, cols(h)], stored.at[h])

    barrier = pltpu.get_barrier_semaphore()

    @pl.when(me > first)
    def _():
        pl.semaphore_signal(
            barrier, inc=1, device_id={"ctx": left}, device_id_type=pl.DeviceIdType.MESH
        )

    @pl.when(me < last)
    def _():
        pl.semaphore_signal(
            barrier, inc=1, device_id={"ctx": right}, device_id_type=pl.DeviceIdType.MESH
        )

    peers = (me > first).astype(jnp.int32) + (me < last).astype(jnp.int32)
    pl.semaphore_wait(barrier, peers)

    key_at = lax.broadcasted_iota(jnp.int32, (tok, tok), 0)
    query_at = lax.broadcasted_iota(jnp.int32, (tok, tok), 1)
    causal = key_at <= query_at

    def soft(scores, values):
        peak = functools.reduce(
            jnp.maximum, [jnp.max(s, axis=0, keepdims=True) for s in scores]
        )
        total, out = 0.0, 0.0
        for s, v in zip(scores, values):
            e = jnp.exp2((s - peak) * EXP_SCALE)
            total = total + jnp.sum(e, axis=0, keepdims=True)
            out = out + tn(v, e.astype(jnp.bfloat16))
        return peak, total, out

    def normalised(soft_sum):
        peak, total, out = soft_sum
        return peak + jnp.log2(total) * (1.0 / EXP_SCALE), out * (1.0 / total)

    def merge(one, level, out):
        top = jnp.maximum(one[0], level)
        f1 = jnp.exp2((one[0] - top) * EXP_SCALE)
        f2 = jnp.exp2((level - top) * EXP_SCALE)
        return top, one[1] * f1 + f2, one[2] * f1 + out.astype(jnp.float32) * f2

    def local_linear(q, phi_k, v):
        phi_q = feature_map(q)
        affinity = jnp.where(causal, nt(phi_k, phi_q), 0.0).astype(jnp.bfloat16)
        return phi_q, tn(v, affinity)

    def finish(h, soft_sum, linear):
        _, total, out = soft_sum
        att = out * (1.0 / total)
        att = att * lax.rsqrt(jnp.mean(att * att, axis=0, keepdims=True) + EPS)
        lin = linear * lax.rsqrt(jnp.mean(linear * linear, axis=0, keepdims=True) + EPS)
        row = att.T * gw_ref[pl.ds(h, 1), :] + lin.T * gn_ref[pl.ds(h, 1), :]
        mixed[:, cols(h)] = row.astype(jnp.bfloat16)
        store(h).start()

    def diagonal(q, k):
        return jnp.where(causal, nt(k, q), LOW)

    @pl.when(me == first)
    def _():
        def start(h):
            k_right(h).start()
            v_right(h).start()

        each_head(start)

        for load in loads:
            load.wait()

        def compute(h):
            q, k, v = q_own[:, cols(h)], k_own[:, cols(h)], v_own[:, cols(h)]
            _, linear = local_linear(q, feature_map(k), v)
            finish(h, soft([diagonal(q, k)], [v]), linear)

        each_head(compute)

        def drain(h):
            k_right(h).wait_send()
            v_right(h).wait_send()

        each_head(drain)

    @pl.when(me == hub)
    def _():
        for load in loads:
            load.wait()

        def compute(h, later_first):
            q, k, v = q_own[:, cols(h)], k_own[:, cols(h)], v_own[:, cols(h)]
            phi_k = feature_map(k)
            state = tn(phi_k, v)
            k_right(h).wait_recv()
            v_right(h).wait_recv()
            k0, v0 = kr[:, cols(h)], vr[:, cols(h)]
            before = tn(feature_map(k0), v0)
            sn_s[h] = (before + state).astype(jnp.bfloat16)
            sn_right(h).start()

            def part(arrival, queries, row, target, sending):
                arrival(h).wait_recv()
                other = queries[:, cols(h)]
                level, out = normalised(soft([nt(k0, other), nt(k, other)], [v0, v]))
                target[h] = out.astype(jnp.bfloat16)
                st_s[h, row : row + 1] = level
                return sending(h)

            part_a = (q_left, qa, 0, oa_s, oa_right)
            part_b = (q_relay, qb, 1, ob_s, ob_right)
            order = (part_b, part_a) if later_first else (part_a, part_b)
            part(*order[0]).start()
            second = part(*order[1])
            st_right(h).start()
            second.start()
            phi_q, linear = local_linear(q, phi_k, v)
            linear = linear + tt(before.astype(jnp.bfloat16), phi_q)
            finish(h, soft([nt(k0, q), diagonal(q, k)], [v0, v]), linear)

        compute(0, False)

        def step(h, carry):
            compute(h, True)
            return carry

        lax.fori_loop(1, heads, step, 0)

        def drain(h):
            st_right(h).wait_send()
            ob_right(h).wait_send()
            sn_right(h).wait_send()
            oa_right(h).wait_send()

        each_head(drain)

    @pl.when((me > hub) & (me < last))
    def _():
        def relay(h):
            q_left(h).start()
            q_left(h).wait_recv()
            q_relay(h).start()

        each_head(relay)

        for load in loads:
            load.wait()

        def compute(h):
            q, k, v = q_own[:, cols(h)], k_own[:, cols(h)], v_own[:, cols(h)]
            phi_k = feature_map(k)
            phi_q, linear = local_linear(q, phi_k, v)
            state = tn(phi_k, v)
            other = soft([nt(k, qa[:, cols(h)])], [v])
            own = soft([diagonal(q, k)], [v])
            sn_right(h).wait_recv()
            carried = sn_r[h]
            sn_s[h] = (carried.astype(jnp.float32) + state).astype(jnp.bfloat16)
            sn_right(h).start()
            linear = linear + tt(carried, phi_q)
            st_right(h).wait_recv()
            ob_right(h).wait_recv()
            level, out = normalised(merge(other, st_r[h, 1:2], ob_r[h]))
            oa_s[h] = out.astype(jnp.bfloat16)
            st_s[h, 0:1] = level
            st_s[h, 1:2] = level
            st_right(h).start()
            oa_right(h).start()
            oa_right(h).wait_recv()
            finish(h, merge(own, st_r[h, 0:1], oa_r[h]), linear)

        each_head(compute)

        def drain(h):
            q_left(h).wait_send()
            q_relay(h).wait_send()
            st_right(h).wait_send()
            oa_right(h).wait_send()
            sn_right(h).wait_send()

        each_head(drain)

    @pl.when(me == last)
    def _():
        def start(h):
            q_left(h).start()

        each_head(start)

        for load in loads:
            load.wait()

        def compute(h):
            q, k, v = q_own[:, cols(h)], k_own[:, cols(h)], v_own[:, cols(h)]
            phi_q, linear = local_linear(q, feature_map(k), v)
            own = soft([diagonal(q, k)], [v])
            sn_right(h).wait_recv()
            linear = linear + tt(sn_r[h], phi_q)
            st_right(h).wait_recv()
            oa_right(h).wait_recv()
            finish(h, merge(own, st_r[h, 0:1], oa_r[h]), linear)

        each_head(compute)

        def drain(h):
            q_left(h).wait_send()

        each_head(drain)

    def settle(h):
        store(h).wait()

    each_head(settle)


def copy_kernel(chunks, src_ref, dst_ref, held, arrived, left):
    rows = held.shape[0] // chunks
    into = [
        pltpu.make_async_copy(
            src_ref.at[pl.ds(i * rows, rows)], held.at[pl.ds(i * rows, rows)], arrived.at[i]
        )
        for i in range(chunks)
    ]
    out = [
        pltpu.make_async_copy(
            held.at[pl.ds(i * rows, rows)], dst_ref.at[pl.ds(i * rows, rows)], left.at[i]
        )
        for i in range(chunks)
    ]
    for one in into:
        one.start()
    for one, other in zip(into, out):
        one.wait()
        other.start()
    for other in out:
        other.wait()


def copied(array, chunks=4):
    hbm = pl.BlockSpec(memory_space=pl.ANY)
    return pl.pallas_call(
        functools.partial(copy_kernel, chunks),
        out_shape=jax.ShapeDtypeStruct(array.shape, array.dtype),
        in_specs=[hbm],
        out_specs=hbm,
        scratch_shapes=[
            pltpu.VMEM(array.shape, array.dtype),
            pltpu.SemaphoreType.DMA((chunks,)),
            pltpu.SemaphoreType.DMA((chunks,)),
        ],
        name="result_copy",
    )(array)


def hub_shards(n, queries, key_vectors, value_vectors, norm_gain, window_gain):
    tok, width = queries.shape
    heads = width // HEAD
    vmem = pl.BlockSpec(memory_space=pltpu.VMEM)
    hbm = pl.BlockSpec(memory_space=pl.ANY)
    block = pltpu.VMEM((tok, width), jnp.bfloat16)
    partial = pltpu.VMEM((heads, HEAD, tok), jnp.bfloat16)
    stats = pltpu.VMEM((heads, 2, tok), jnp.float32)
    state = pltpu.VMEM((heads, HEAD, HEAD), jnp.bfloat16)
    return pl.pallas_call(
        functools.partial(hub_kernel, n),
        out_shape=jax.ShapeDtypeStruct((tok, width), jnp.bfloat16),
        in_specs=[hbm] * 3 + [vmem] * 2,
        out_specs=hbm,
        scratch_shapes=[block] * 4
        + [partial, partial, stats, state] * 2
        + [block] * 4
        + [pltpu.SemaphoreType.DMA((8, heads)), pltpu.SemaphoreType.DMA((8, heads))]
        + [pltpu.SemaphoreType.DMA((3,)), pltpu.SemaphoreType.DMA((heads,))],
        compiler_params=pltpu.CompilerParams(
            collective_id=0, has_side_effects=True, vmem_limit_bytes=56 * 2**20
        ),
        name="hub_attention",
    )(
        queries,
        key_vectors,
        value_vectors,
        norm_gain.reshape(heads, HEAD),
        window_gain.reshape(heads, HEAD),
    )


def solution(mesh):
    count = mesh.shape["ctx"]

    def run(queries, key_vectors, value_vectors, norm_gain, window_gain):
        args = (queries, key_vectors, value_vectors, norm_gain, window_gain)
        fits = count * queries.shape[0] <= WINDOW
        if fits and count - 2 == 2:
            return copied(hub_shards(count, *args))
        return shards(*args)

    return jax.shard_map(
        run,
        mesh=mesh,
        in_specs=(P(("dp", "ctx"), None), P(("dp", "ctx"), None), P(("dp", "ctx"), None), P(), P()),
        out_specs=P(("dp", "ctx"), None),
        check_vma=False,
    )
```

```python
import functools
import math

import jax
import jax.numpy as jnp
from jax import lax
from jax.experimental import pallas as pl
from jax.experimental.pallas import tpu as pltpu
from jax.sharding import PartitionSpec as P

HEAD = 128
WINDOW = 1024
EPS = 1e-05


def passed_along(value, axis, steps):
    count = lax.axis_size(axis)
    leading, last = (max(0, -steps), min(count, count - steps))
    return lax.ppermute(value, axis, [(source, source + steps) for source in range(leading, last)])


def entering(array, axis, combine, identity):
    peers, position = (lax.axis_size(axis), lax.axis_index(axis))
    everything = lax.all_gather(array.astype(jnp.bfloat16), axis)
    start = jnp.broadcast_to(jnp.asarray(identity, array.dtype), array.shape)

    def lap(k, before):
        reached = k < position
        new = combine(before, everything[k].astype(array.dtype))
        return jnp.where(reached, new, before)

    return lax.fori_loop(0, peers, lap, start)


def feature_map(values):
    upcast = values.astype(jnp.float32)
    return jnp.where(upcast > 0, upcast + 1.0, jnp.exp(jnp.minimum(upcast, 0.0))).astype(
        jnp.bfloat16
    )


def add_states(earlier, later):
    return earlier + later


def shards(queries, key_vectors, value_vectors, norm_gain, window_gain):
    tok_rows, model_width = queries.shape
    head_count = model_width // HEAD
    ctx_index = lax.axis_index("ctx")
    reach_blocks = WINDOW // tok_rows
    own_pair = (key_vectors, value_vectors)
    received = []
    travelling = own_pair
    for distance in range(reach_blocks):
        travelling = passed_along((travelling[0], travelling[1]), "ctx", 1)
        received.append(travelling)
    ordered = received[::-1] + [own_pair]
    window_keys = jnp.concatenate([member[0] for member in ordered], axis=0)
    window_values = jnp.concatenate([member[1] for member in ordered], axis=0)
    span_rows = window_keys.shape[0]
    query_place = ctx_index * tok_rows + jnp.arange(tok_rows, dtype=jnp.int32)
    key_place = (ctx_index - reach_blocks) * tok_rows + jnp.arange(span_rows, dtype=jnp.int32)
    inside = (
        (key_place[None, :] <= query_place[:, None])
        & (query_place[:, None] - key_place[None, :] < WINDOW)
        & (key_place[None, :] >= 0)
    )
    group_size = 4
    groups = head_count // group_size
    scale = 1.0 / math.sqrt(HEAD)

    def split_groups(matrix):
        return jnp.moveaxis(matrix.reshape(matrix.shape[0], groups, group_size, HEAD), 1, 0)

    def attend(operands):
        query_group, key_group, value_group = operands
        scores = (
            jnp.einsum("tge,sge->gts", query_group, key_group, preferred_element_type=jnp.float32)
            * scale
        )
        scores = jnp.where(inside[None], scores, -jnp.inf)
        peak = jnp.max(scores, axis=-1, keepdims=True)
        expos = jnp.exp(scores - peak)
        weights = (expos / jnp.sum(expos, axis=-1, keepdims=True)).astype(jnp.bfloat16)
        return jnp.einsum("gts,sge->tge", weights, value_group, preferred_element_type=jnp.float32)

    attended = lax.map(
        attend, (split_groups(queries), split_groups(window_keys), split_groups(window_values))
    )
    attended = jnp.moveaxis(attended, 0, 1).reshape(tok_rows, head_count, HEAD)
    windowed = attended * lax.rsqrt(jnp.mean(attended * attended, axis=-1, keepdims=True) + EPS)
    windowed = windowed * window_gain.reshape(head_count, HEAD)
    phi_query = feature_map(queries).reshape(tok_rows, head_count, HEAD)
    phi_key = feature_map(key_vectors).reshape(tok_rows, head_count, HEAD)
    value_heads = value_vectors.reshape(tok_rows, head_count, HEAD)
    local_state = jnp.einsum(
        "the,thf->hef", phi_key, value_heads, preferred_element_type=jnp.float32
    )
    carried = entering(local_state, "ctx", add_states, jnp.zeros_like(local_state))
    from_state = jnp.einsum(
        "the,hef->thf", phi_query, carried.astype(jnp.bfloat16), preferred_element_type=jnp.float32
    )
    affinity = jnp.einsum("the,she->hts", phi_query, phi_key, preferred_element_type=jnp.float32)
    inner = jnp.arange(tok_rows, dtype=jnp.int32)
    causal = inner[:, None] >= inner[None, :]
    affinity = jnp.where(causal[None], affinity, 0.0).astype(jnp.bfloat16)
    local_part = jnp.einsum(
        "hts,shf->thf", affinity, value_heads, preferred_element_type=jnp.float32
    )
    linear = from_state + local_part
    normed = linear * lax.rsqrt(jnp.mean(linear * linear, axis=-1, keepdims=True) + EPS)
    normed = normed * norm_gain.reshape(head_count, HEAD)
    return (windowed + normed).reshape(tok_rows, model_width).astype(jnp.bfloat16)


QA, QB, KK, VV, OA, OB, ST, SN = range(8)
EXP_SCALE = math.log2(math.e) / math.sqrt(HEAD)
LOW = -1e30


def nt(a, b):
    return lax.dot_general(a, b, (((1,), (1,)), ((), ())), preferred_element_type=jnp.float32)


def tn(a, b):
    return lax.dot_general(a, b, (((0,), (0,)), ((), ())), preferred_element_type=jnp.float32)


def tt(a, b):
    return lax.dot_general(a, b, (((0,), (1,)), ((), ())), preferred_element_type=jnp.float32)


def hub_kernel(
    n,
    q_ref, k_ref, v_ref, gn_ref, gw_ref, out_ref,
    qa, qb, kr, vr, oa_s, ob_s, st_s, sn_s, oa_r, ob_r, st_r, sn_r,
    q_own, k_own, v_own, mixed, send, recv, loaded, stored,
):
    tok, width = q_ref.shape
    heads = width // HEAD
    me = lax.axis_index("ctx")
    left, right = me - 1, me + 1
    first, hub, last = 0, 1, n - 1

    def cols(h):
        return pl.ds(pl.multiple_of(h * HEAD, HEAD), HEAD)

    def move(stream, src, dst, h, target):
        return pltpu.make_async_remote_copy(
            src_ref=src,
            dst_ref=dst,
            send_sem=send.at[stream, h],
            recv_sem=recv.at[stream, h],
            device_id={"ctx": target},
            device_id_type=pl.DeviceIdType.MESH,
        )

    def q_left(h):
        return move(QA, q_ref.at[:, cols(h)], qa.at[:, cols(h)], h, left)

    def q_relay(h):
        return move(QB, qa.at[:, cols(h)], qb.at[:, cols(h)], h, left)

    def k_right(h):
        return move(KK, k_ref.at[:, cols(h)], kr.at[:, cols(h)], h, right)

    def v_right(h):
        return move(VV, v_ref.at[:, cols(h)], vr.at[:, cols(h)], h, right)

    def oa_right(h):
        return move(OA, oa_s.at[h], oa_r.at[h], h, right)

    def ob_right(h):
        return move(OB, ob_s.at[h], ob_r.at[h], h, right)

    def st_right(h):
        return move(ST, st_s.at[h], st_r.at[h], h, right)

    def sn_right(h):
        return move(SN, sn_s.at[h], sn_r.at[h], h, right)

    def each_head(body):
        def step(h, carry):
            body(h)
            return carry

        lax.fori_loop(0, heads, step, 0)

    loads = [
        pltpu.make_async_copy(src, dst, loaded.at[i])
        for i, (src, dst) in enumerate([(k_ref, k_own), (v_ref, v_own), (q_ref, q_own)])
    ]
    for load in loads:
        load.start()

    def store(h):
        return pltpu.make_async_copy(mixed.at[:, cols(h)], out_ref.at[:, cols(h)], stored.at[h])

    barrier = pltpu.get_barrier_semaphore()

    @pl.when(me > first)
    def _():
        pl.semaphore_signal(
            barrier, inc=1, device_id={"ctx": left}, device_id_type=pl.DeviceIdType.MESH
        )

    @pl.when(me < last)
    def _():
        pl.semaphore_signal(
            barrier, inc=1, device_id={"ctx": right}, device_id_type=pl.DeviceIdType.MESH
        )

    peers = (me > first).astype(jnp.int32) + (me < last).astype(jnp.int32)
    pl.semaphore_wait(barrier, peers)

    key_at = lax.broadcasted_iota(jnp.int32, (tok, tok), 0)
    query_at = lax.broadcasted_iota(jnp.int32, (tok, tok), 1)
    causal = key_at <= query_at

    def soft(scores, values):
        peak = functools.reduce(
            jnp.maximum, [jnp.max(s, axis=0, keepdims=True) for s in scores]
        )
        total, out = 0.0, 0.0
        for s, v in zip(scores, values):
            e = jnp.exp2((s - peak) * EXP_SCALE)
            total = total + jnp.sum(e, axis=0, keepdims=True)
            out = out + tn(v, e.astype(jnp.bfloat16))
        return peak, total, out

    def normalised(soft_sum):
        peak, total, out = soft_sum
        return peak + jnp.log2(total) * (1.0 / EXP_SCALE), out * (1.0 / total)

    def merge(one, level, out):
        top = jnp.maximum(one[0], level)
        f1 = jnp.exp2((one[0] - top) * EXP_SCALE)
        f2 = jnp.exp2((level - top) * EXP_SCALE)
        return top, one[1] * f1 + f2, one[2] * f1 + out.astype(jnp.float32) * f2

    def local_linear(q, phi_k, v):
        phi_q = feature_map(q)
        affinity = jnp.where(causal, nt(phi_k, phi_q), 0.0).astype(jnp.bfloat16)
        return phi_q, tn(v, affinity)

    def finish(h, soft_sum, linear):
        _, total, out = soft_sum
        att = out * (1.0 / total)
        att = att * lax.rsqrt(jnp.mean(att * att, axis=0, keepdims=True) + EPS)
        lin = linear * lax.rsqrt(jnp.mean(linear * linear, axis=0, keepdims=True) + EPS)
        row = att.T * gw_ref[pl.ds(h, 1), :] + lin.T * gn_ref[pl.ds(h, 1), :]
        mixed[:, cols(h)] = row.astype(jnp.bfloat16)
        store(h).start()

    def diagonal(q, k):
        return jnp.where(causal, nt(k, q), LOW)

    @pl.when(me == first)
    def _():
        def start(h):
            k_right(h).start()
            v_right(h).start()

        each_head(start)

        for load in loads:
            load.wait()

        def compute(h):
            q, k, v = q_own[:, cols(h)], k_own[:, cols(h)], v_own[:, cols(h)]
            _, linear = local_linear(q, feature_map(k), v)
            finish(h, soft([diagonal(q, k)], [v]), linear)

        each_head(compute)

        def drain(h):
            k_right(h).wait_send()
            v_right(h).wait_send()

        each_head(drain)

    @pl.when(me == hub)
    def _():
        for load in loads:
            load.wait()

        def compute(h, later_first):
            q, k, v = q_own[:, cols(h)], k_own[:, cols(h)], v_own[:, cols(h)]
            phi_k = feature_map(k)
            state = tn(phi_k, v)
            k_right(h).wait_recv()
            v_right(h).wait_recv()
            k0, v0 = kr[:, cols(h)], vr[:, cols(h)]
            before = tn(feature_map(k0), v0)
            sn_s[h] = (before + state).astype(jnp.bfloat16)
            sn_right(h).start()

            def part(arrival, queries, row, target, sending):
                arrival(h).wait_recv()
                other = queries[:, cols(h)]
                level, out = normalised(soft([nt(k0, other), nt(k, other)], [v0, v]))
                target[h] = out.astype(jnp.bfloat16)
                st_s[h, row : row + 1] = level
                return sending(h)

            part_a = (q_left, qa, 0, oa_s, oa_right)
            part_b = (q_relay, qb, 1, ob_s, ob_right)
            if later_first:
                part(*part_b).start()

                @pl.when(h > 1)
                def _():
                    oa_right(h - 1).start()

                part(*part_a)
                st_right(h).start()
            else:
                part(*part_a).start()
                part(*part_b).start()
                st_right(h).start()
            phi_q, linear = local_linear(q, phi_k, v)
            linear = linear + tt(before.astype(jnp.bfloat16), phi_q)
            finish(h, soft([nt(k0, q), diagonal(q, k)], [v0, v]), linear)

        compute(0, False)

        def step(h, carry):
            compute(h, True)
            return carry

        lax.fori_loop(1, heads, step, 0)
        oa_right(heads - 1).start()

        def drain(h):
            st_right(h).wait_send()
            ob_right(h).wait_send()
            sn_right(h).wait_send()
            oa_right(h).wait_send()

        each_head(drain)

    @pl.when((me > hub) & (me < last))
    def _():
        def relay(h):
            q_left(h).start()
            q_left(h).wait_recv()
            q_relay(h).start()

        each_head(relay)

        for load in loads:
            load.wait()

        def front(h):
            q, k, v = q_own[:, cols(h)], k_own[:, cols(h)], v_own[:, cols(h)]
            phi_k = feature_map(k)
            phi_q, linear = local_linear(q, phi_k, v)
            state = tn(phi_k, v)
            other = soft([nt(k, qa[:, cols(h)])], [v])
            own = soft([diagonal(q, k)], [v])
            sn_right(h).wait_recv()
            carried = sn_r[h]
            sn_s[h] = (carried.astype(jnp.float32) + state).astype(jnp.bfloat16)
            sn_right(h).start()
            linear = linear + tt(carried, phi_q)
            st_right(h).wait_recv()
            ob_right(h).wait_recv()
            level, out = normalised(merge(other, st_r[h, 1:2], ob_r[h]))
            oa_s[h] = out.astype(jnp.bfloat16)
            st_s[h, 0:1] = level
            st_s[h, 1:2] = level
            st_right(h).start()
            oa_right(h).start()
            return own, linear

        def back(h, held):
            own, linear = held
            oa_right(h).wait_recv()
            finish(h, merge(own, st_r[h, 0:1], oa_r[h]), linear)

        def step(h, held):
            ahead = front(h)
            back(h - 1, held)
            return ahead

        back(heads - 1, lax.fori_loop(1, heads, step, front(0)))

        def drain(h):
            q_left(h).wait_send()
            q_relay(h).wait_send()
            st_right(h).wait_send()
            oa_right(h).wait_send()
            sn_right(h).wait_send()

        each_head(drain)

    @pl.when(me == last)
    def _():
        def start(h):
            q_left(h).start()

        each_head(start)

        for load in loads:
            load.wait()

        def compute(h):
            q, k, v = q_own[:, cols(h)], k_own[:, cols(h)], v_own[:, cols(h)]
            phi_q, linear = local_linear(q, feature_map(k), v)
            own = soft([diagonal(q, k)], [v])
            sn_right(h).wait_recv()
            linear = linear + tt(sn_r[h], phi_q)
            st_right(h).wait_recv()
            oa_right(h).wait_recv()
            finish(h, merge(own, st_r[h, 0:1], oa_r[h]), linear)

        each_head(compute)

        def drain(h):
            q_left(h).wait_send()

        each_head(drain)

    def settle(h):
        store(h).wait()

    each_head(settle)


def copy_kernel(chunks, src_ref, dst_ref, held, arrived, left):
    rows = held.shape[0] // chunks
    into = [
        pltpu.make_async_copy(
            src_ref.at[pl.ds(i * rows, rows)], held.at[pl.ds(i * rows, rows)], arrived.at[i]
        )
        for i in range(chunks)
    ]
    out = [
        pltpu.make_async_copy(
            held.at[pl.ds(i * rows, rows)], dst_ref.at[pl.ds(i * rows, rows)], left.at[i]
        )
        for i in range(chunks)
    ]
    for one in into:
        one.start()
    for one, other in zip(into, out):
        one.wait()
        other.start()
    for other in out:
        other.wait()


def copied(array, chunks=4):
    hbm = pl.BlockSpec(memory_space=pl.ANY)
    return pl.pallas_call(
        functools.partial(copy_kernel, chunks),
        out_shape=jax.ShapeDtypeStruct(array.shape, array.dtype),
        in_specs=[hbm],
        out_specs=hbm,
        scratch_shapes=[
            pltpu.VMEM(array.shape, array.dtype),
            pltpu.SemaphoreType.DMA((chunks,)),
            pltpu.SemaphoreType.DMA((chunks,)),
        ],
        name="result_copy",
    )(array)


def hub_shards(n, queries, key_vectors, value_vectors, norm_gain, window_gain):
    tok, width = queries.shape
    heads = width // HEAD
    vmem = pl.BlockSpec(memory_space=pltpu.VMEM)
    hbm = pl.BlockSpec(memory_space=pl.ANY)
    block = pltpu.VMEM((tok, width), jnp.bfloat16)
    partial = pltpu.VMEM((heads, HEAD, tok), jnp.bfloat16)
    stats = pltpu.VMEM((heads, 2, tok), jnp.float32)
    state = pltpu.VMEM((heads, HEAD, HEAD), jnp.bfloat16)
    return pl.pallas_call(
        functools.partial(hub_kernel, n),
        out_shape=jax.ShapeDtypeStruct((tok, width), jnp.bfloat16),
        in_specs=[hbm] * 3 + [vmem] * 2,
        out_specs=hbm,
        scratch_shapes=[block] * 4
        + [partial, partial, stats, state] * 2
        + [block] * 4
        + [pltpu.SemaphoreType.DMA((8, heads)), pltpu.SemaphoreType.DMA((8, heads))]
        + [pltpu.SemaphoreType.DMA((3,)), pltpu.SemaphoreType.DMA((heads,))],
        compiler_params=pltpu.CompilerParams(
            collective_id=0, has_side_effects=True, vmem_limit_bytes=56 * 2**20
        ),
        name="hub_attention",
    )(
        queries,
        key_vectors,
        value_vectors,
        norm_gain.reshape(heads, HEAD),
        window_gain.reshape(heads, HEAD),
    )


def solution(mesh):
    count = mesh.shape["ctx"]

    def run(queries, key_vectors, value_vectors, norm_gain, window_gain):
        args = (queries, key_vectors, value_vectors, norm_gain, window_gain)
        fits = count * queries.shape[0] <= WINDOW
        if fits and count - 2 == 2:
            return copied(hub_shards(count, *args))
        return shards(*args)

    return jax.shard_map(
        run,
        mesh=mesh,
        in_specs=(P(("dp", "ctx"), None), P(("dp", "ctx"), None), P(("dp", "ctx"), None), P(), P()),
        out_specs=P(("dp", "ctx"), None),
        check_vma=False,
    )
```

```python
import functools
import math

import jax
import jax.numpy as jnp
from jax import lax
from jax.experimental import pallas as pl
from jax.experimental.pallas import tpu as pltpu
from jax.sharding import PartitionSpec as P

HEAD = 128
WINDOW = 1024
EPS = 1e-05


def passed_along(value, axis, steps):
    count = lax.axis_size(axis)
    leading, last = (max(0, -steps), min(count, count - steps))
    return lax.ppermute(value, axis, [(source, source + steps) for source in range(leading, last)])


def entering(array, axis, combine, identity):
    peers, position = (lax.axis_size(axis), lax.axis_index(axis))
    everything = lax.all_gather(array.astype(jnp.bfloat16), axis)
    start = jnp.broadcast_to(jnp.asarray(identity, array.dtype), array.shape)

    def lap(k, before):
        reached = k < position
        new = combine(before, everything[k].astype(array.dtype))
        return jnp.where(reached, new, before)

    return lax.fori_loop(0, peers, lap, start)


def feature_map(values):
    upcast = values.astype(jnp.float32)
    return jnp.where(upcast > 0, upcast + 1.0, jnp.exp(jnp.minimum(upcast, 0.0))).astype(
        jnp.bfloat16
    )


def add_states(earlier, later):
    return earlier + later


def shards(queries, key_vectors, value_vectors, norm_gain, window_gain):
    tok_rows, model_width = queries.shape
    head_count = model_width // HEAD
    ctx_index = lax.axis_index("ctx")
    reach_blocks = WINDOW // tok_rows
    own_pair = (key_vectors, value_vectors)
    received = []
    travelling = own_pair
    for distance in range(reach_blocks):
        travelling = passed_along((travelling[0], travelling[1]), "ctx", 1)
        received.append(travelling)
    ordered = received[::-1] + [own_pair]
    window_keys = jnp.concatenate([member[0] for member in ordered], axis=0)
    window_values = jnp.concatenate([member[1] for member in ordered], axis=0)
    span_rows = window_keys.shape[0]
    query_place = ctx_index * tok_rows + jnp.arange(tok_rows, dtype=jnp.int32)
    key_place = (ctx_index - reach_blocks) * tok_rows + jnp.arange(span_rows, dtype=jnp.int32)
    inside = (
        (key_place[None, :] <= query_place[:, None])
        & (query_place[:, None] - key_place[None, :] < WINDOW)
        & (key_place[None, :] >= 0)
    )
    group_size = 4
    groups = head_count // group_size
    scale = 1.0 / math.sqrt(HEAD)

    def split_groups(matrix):
        return jnp.moveaxis(matrix.reshape(matrix.shape[0], groups, group_size, HEAD), 1, 0)

    def attend(operands):
        query_group, key_group, value_group = operands
        scores = (
            jnp.einsum("tge,sge->gts", query_group, key_group, preferred_element_type=jnp.float32)
            * scale
        )
        scores = jnp.where(inside[None], scores, -jnp.inf)
        peak = jnp.max(scores, axis=-1, keepdims=True)
        expos = jnp.exp(scores - peak)
        weights = (expos / jnp.sum(expos, axis=-1, keepdims=True)).astype(jnp.bfloat16)
        return jnp.einsum("gts,sge->tge", weights, value_group, preferred_element_type=jnp.float32)

    attended = lax.map(
        attend, (split_groups(queries), split_groups(window_keys), split_groups(window_values))
    )
    attended = jnp.moveaxis(attended, 0, 1).reshape(tok_rows, head_count, HEAD)
    windowed = attended * lax.rsqrt(jnp.mean(attended * attended, axis=-1, keepdims=True) + EPS)
    windowed = windowed * window_gain.reshape(head_count, HEAD)
    phi_query = feature_map(queries).reshape(tok_rows, head_count, HEAD)
    phi_key = feature_map(key_vectors).reshape(tok_rows, head_count, HEAD)
    value_heads = value_vectors.reshape(tok_rows, head_count, HEAD)
    local_state = jnp.einsum(
        "the,thf->hef", phi_key, value_heads, preferred_element_type=jnp.float32
    )
    carried = entering(local_state, "ctx", add_states, jnp.zeros_like(local_state))
    from_state = jnp.einsum(
        "the,hef->thf", phi_query, carried.astype(jnp.bfloat16), preferred_element_type=jnp.float32
    )
    affinity = jnp.einsum("the,she->hts", phi_query, phi_key, preferred_element_type=jnp.float32)
    inner = jnp.arange(tok_rows, dtype=jnp.int32)
    causal = inner[:, None] >= inner[None, :]
    affinity = jnp.where(causal[None], affinity, 0.0).astype(jnp.bfloat16)
    local_part = jnp.einsum(
        "hts,shf->thf", affinity, value_heads, preferred_element_type=jnp.float32
    )
    linear = from_state + local_part
    normed = linear * lax.rsqrt(jnp.mean(linear * linear, axis=-1, keepdims=True) + EPS)
    normed = normed * norm_gain.reshape(head_count, HEAD)
    return (windowed + normed).reshape(tok_rows, model_width).astype(jnp.bfloat16)


QA, QB, KK, VV, OA, OB, ST, SN = range(8)
EXP_SCALE = math.log2(math.e) / math.sqrt(HEAD)
LOW = -1e30


def nt(a, b):
    return lax.dot_general(a, b, (((1,), (1,)), ((), ())), preferred_element_type=jnp.float32)


def tn(a, b):
    return lax.dot_general(a, b, (((0,), (0,)), ((), ())), preferred_element_type=jnp.float32)


def tt(a, b):
    return lax.dot_general(a, b, (((0,), (1,)), ((), ())), preferred_element_type=jnp.float32)


def hub_kernel(
    n,
    q_ref, k_ref, v_ref, gn_ref, gw_ref, out_ref,
    qa, qb, kr, vr, oa_s, ob_s, st_s, sn_s, oa_r, ob_r, st_r, sn_r,
    q_own, k_own, v_own, send, recv, loaded,
):
    tok, width = q_ref.shape
    heads = width // HEAD
    me = lax.axis_index("ctx")
    left, right = me - 1, me + 1
    first, hub, last = 0, 1, n - 1

    def cols(h):
        return pl.ds(pl.multiple_of(h * HEAD, HEAD), HEAD)

    def move(stream, src, dst, h, target):
        return pltpu.make_async_remote_copy(
            src_ref=src,
            dst_ref=dst,
            send_sem=send.at[stream, h],
            recv_sem=recv.at[stream, h],
            device_id={"ctx": target},
            device_id_type=pl.DeviceIdType.MESH,
        )

    def q_left(h):
        return move(QA, q_ref.at[:, cols(h)], qa.at[:, cols(h)], h, left)

    def q_relay(h):
        return move(QB, qa.at[:, cols(h)], qb.at[:, cols(h)], h, left)

    def k_right(h):
        return move(KK, k_ref.at[:, cols(h)], kr.at[:, cols(h)], h, right)

    def v_right(h):
        return move(VV, v_ref.at[:, cols(h)], vr.at[:, cols(h)], h, right)

    def oa_right(h):
        return move(OA, oa_s.at[h], oa_r.at[h], h, right)

    def ob_right(h):
        return move(OB, ob_s.at[h], ob_r.at[h], h, right)

    def st_right(h):
        return move(ST, st_s.at[h], st_r.at[h], h, right)

    def sn_right(h):
        return move(SN, sn_s.at[h], sn_r.at[h], h, right)

    def each_head(body):
        def step(h, carry):
            body(h)
            return carry

        lax.fori_loop(0, heads, step, 0)

    loads = [
        pltpu.make_async_copy(src, dst, loaded.at[i])
        for i, (src, dst) in enumerate([(k_ref, k_own), (v_ref, v_own), (q_ref, q_own)])
    ]
    for load in loads:
        load.start()

    barrier = pltpu.get_barrier_semaphore()

    @pl.when(me > first)
    def _():
        pl.semaphore_signal(
            barrier, inc=1, device_id={"ctx": left}, device_id_type=pl.DeviceIdType.MESH
        )

    @pl.when(me < last)
    def _():
        pl.semaphore_signal(
            barrier, inc=1, device_id={"ctx": right}, device_id_type=pl.DeviceIdType.MESH
        )

    peers = (me > first).astype(jnp.int32) + (me < last).astype(jnp.int32)
    pl.semaphore_wait(barrier, peers)

    key_at = lax.broadcasted_iota(jnp.int32, (tok, tok), 0)
    query_at = lax.broadcasted_iota(jnp.int32, (tok, tok), 1)
    causal = key_at <= query_at

    def soft(scores, values):
        peak = functools.reduce(
            jnp.maximum, [jnp.max(s, axis=0, keepdims=True) for s in scores]
        )
        total, out = 0.0, 0.0
        for s, v in zip(scores, values):
            e = jnp.exp2((s - peak) * EXP_SCALE)
            total = total + jnp.sum(e, axis=0, keepdims=True)
            out = out + tn(v, e.astype(jnp.bfloat16))
        return peak, total, out

    def normalised(soft_sum):
        peak, total, out = soft_sum
        return peak + jnp.log2(total) * (1.0 / EXP_SCALE), out * (1.0 / total)

    def merge(one, level, out):
        top = jnp.maximum(one[0], level)
        f1 = jnp.exp2((one[0] - top) * EXP_SCALE)
        f2 = jnp.exp2((level - top) * EXP_SCALE)
        return top, one[1] * f1 + f2, one[2] * f1 + out.astype(jnp.float32) * f2

    def local_linear(q, phi_k, v):
        phi_q = feature_map(q)
        affinity = jnp.where(causal, nt(phi_k, phi_q), 0.0).astype(jnp.bfloat16)
        return phi_q, tn(v, affinity)

    def finish(h, soft_sum, linear):
        _, total, out = soft_sum
        att = out * (1.0 / total)
        att = att * lax.rsqrt(jnp.mean(att * att, axis=0, keepdims=True) + EPS)
        lin = linear * lax.rsqrt(jnp.mean(linear * linear, axis=0, keepdims=True) + EPS)
        row = att.T * gw_ref[pl.ds(h, 1), :] + lin.T * gn_ref[pl.ds(h, 1), :]
        out_ref[:, cols(h)] = row.astype(jnp.bfloat16)

    def diagonal(q, k):
        return jnp.where(causal, nt(k, q), LOW)

    @pl.when(me == first)
    def _():
        def start(h):
            k_right(h).start()
            v_right(h).start()

        each_head(start)

        for load in loads:
            load.wait()

        def compute(h):
            q, k, v = q_own[:, cols(h)], k_own[:, cols(h)], v_own[:, cols(h)]
            _, linear = local_linear(q, feature_map(k), v)
            finish(h, soft([diagonal(q, k)], [v]), linear)

        each_head(compute)

        def drain(h):
            k_right(h).wait_send()
            v_right(h).wait_send()

        each_head(drain)

    @pl.when(me == hub)
    def _():
        for load in loads:
            load.wait()

        def compute(h, later_first):
            q, k, v = q_own[:, cols(h)], k_own[:, cols(h)], v_own[:, cols(h)]
            phi_k = feature_map(k)
            state = tn(phi_k, v)
            k_right(h).wait_recv()
            v_right(h).wait_recv()
            k0, v0 = kr[:, cols(h)], vr[:, cols(h)]
            before = tn(feature_map(k0), v0)
            sn_s[h] = (before + state).astype(jnp.bfloat16)
            sn_right(h).start()

            def part(arrival, queries, row, target, sending):
                arrival(h).wait_recv()
                other = queries[:, cols(h)]
                level, out = normalised(soft([nt(k0, other), nt(k, other)], [v0, v]))
                target[h] = out.astype(jnp.bfloat16)
                st_s[h, row : row + 1] = level
                return sending(h)

            part_a = (q_left, qa, 0, oa_s, oa_right)
            part_b = (q_relay, qb, 1, ob_s, ob_right)
            order = (part_b, part_a) if later_first else (part_a, part_b)
            part(*order[0]).start()
            second = part(*order[1])
            st_right(h).start()
            second.start()
            phi_q, linear = local_linear(q, phi_k, v)
            linear = linear + tt(before.astype(jnp.bfloat16), phi_q)
            finish(h, soft([nt(k0, q), diagonal(q, k)], [v0, v]), linear)

        compute(0, False)

        def step(h, carry):
            compute(h, True)
            return carry

        lax.fori_loop(1, heads, step, 0)

        def drain(h):
            st_right(h).wait_send()
            ob_right(h).wait_send()
            sn_right(h).wait_send()
            oa_right(h).wait_send()

        each_head(drain)

    @pl.when((me > hub) & (me < last))
    def _():
        def relay(h):
            q_left(h).start()
            q_left(h).wait_recv()
            q_relay(h).start()

        each_head(relay)

        for load in loads:
            load.wait()

        def compute(h):
            q, k, v = q_own[:, cols(h)], k_own[:, cols(h)], v_own[:, cols(h)]
            phi_k = feature_map(k)
            phi_q, linear = local_linear(q, phi_k, v)
            state = tn(phi_k, v)
            other = soft([nt(k, qa[:, cols(h)])], [v])
            own = soft([diagonal(q, k)], [v])
            sn_right(h).wait_recv()
            carried = sn_r[h]
            sn_s[h] = (carried.astype(jnp.float32) + state).astype(jnp.bfloat16)
            sn_right(h).start()
            linear = linear + tt(carried, phi_q)
            st_right(h).wait_recv()
            ob_right(h).wait_recv()
            level, out = normalised(merge(other, st_r[h, 1:2], ob_r[h]))
            oa_s[h] = out.astype(jnp.bfloat16)
            st_s[h, 0:1] = level
            st_s[h, 1:2] = level
            st_right(h).start()
            oa_right(h).start()
            oa_right(h).wait_recv()
            finish(h, merge(own, st_r[h, 0:1], oa_r[h]), linear)

        each_head(compute)

        def drain(h):
            q_left(h).wait_send()
            q_relay(h).wait_send()
            st_right(h).wait_send()
            oa_right(h).wait_send()
            sn_right(h).wait_send()

        each_head(drain)

    @pl.when(me == last)
    def _():
        def start(h):
            q_left(h).start()

        each_head(start)

        for load in loads:
            load.wait()

        def compute(h):
            q, k, v = q_own[:, cols(h)], k_own[:, cols(h)], v_own[:, cols(h)]
            phi_q, linear = local_linear(q, feature_map(k), v)
            own = soft([diagonal(q, k)], [v])
            sn_right(h).wait_recv()
            linear = linear + tt(sn_r[h], phi_q)
            st_right(h).wait_recv()
            oa_right(h).wait_recv()
            finish(h, merge(own, st_r[h, 0:1], oa_r[h]), linear)

        each_head(compute)

        def drain(h):
            q_left(h).wait_send()

        each_head(drain)


def hub_shards(n, queries, key_vectors, value_vectors, norm_gain, window_gain):
    tok, width = queries.shape
    heads = width // HEAD
    vmem = pl.BlockSpec(memory_space=pltpu.VMEM)
    hbm = pl.BlockSpec(memory_space=pl.ANY)
    block = pltpu.VMEM((tok, width), jnp.bfloat16)
    partial = pltpu.VMEM((heads, HEAD, tok), jnp.bfloat16)
    stats = pltpu.VMEM((heads, 2, tok), jnp.float32)
    state = pltpu.VMEM((heads, HEAD, HEAD), jnp.bfloat16)
    return pl.pallas_call(
        functools.partial(hub_kernel, n),
        out_shape=pltpu.VMEM((tok, width), jnp.bfloat16),
        in_specs=[hbm] * 3 + [vmem] * 2,
        out_specs=vmem,
        scratch_shapes=[block] * 4
        + [partial, partial, stats, state] * 2
        + [block] * 3
        + [pltpu.SemaphoreType.DMA((8, heads)), pltpu.SemaphoreType.DMA((8, heads))]
        + [pltpu.SemaphoreType.DMA((3,))],
        compiler_params=pltpu.CompilerParams(
            collective_id=0, has_side_effects=True, vmem_limit_bytes=56 * 2**20
        ),
        name="hub_attention",
    )(
        queries,
        key_vectors,
        value_vectors,
        norm_gain.reshape(heads, HEAD),
        window_gain.reshape(heads, HEAD),
    )


def solution(mesh):
    count = mesh.shape["ctx"]

    def run(queries, key_vectors, value_vectors, norm_gain, window_gain):
        args = (queries, key_vectors, value_vectors, norm_gain, window_gain)
        fits = count * queries.shape[0] <= WINDOW
        if fits and count - 2 == 2:
            return hub_shards(count, *args)
        return shards(*args)

    return jax.shard_map(
        run,
        mesh=mesh,
        in_specs=(P(("dp", "ctx"), None), P(("dp", "ctx"), None), P(("dp", "ctx"), None), P(), P()),
        out_specs=P(("dp", "ctx"), None),
        check_vma=False,
    )
```

```python
import functools
import math

import jax
import jax.numpy as jnp
from jax import lax
from jax.experimental import pallas as pl
from jax.experimental.pallas import tpu as pltpu
from jax.sharding import PartitionSpec as P

HEAD = 128
WINDOW = 1024
EPS = 1e-05


def passed_along(value, axis, steps):
    count = lax.axis_size(axis)
    leading, last = (max(0, -steps), min(count, count - steps))
    return lax.ppermute(value, axis, [(source, source + steps) for source in range(leading, last)])


def entering(array, axis, combine, identity):
    peers, position = (lax.axis_size(axis), lax.axis_index(axis))
    everything = lax.all_gather(array.astype(jnp.bfloat16), axis)
    start = jnp.broadcast_to(jnp.asarray(identity, array.dtype), array.shape)

    def lap(k, before):
        reached = k < position
        new = combine(before, everything[k].astype(array.dtype))
        return jnp.where(reached, new, before)

    return lax.fori_loop(0, peers, lap, start)


def feature_map(values):
    upcast = values.astype(jnp.float32)
    return jnp.where(upcast > 0, upcast + 1.0, jnp.exp(jnp.minimum(upcast, 0.0))).astype(
        jnp.bfloat16
    )


def add_states(earlier, later):
    return earlier + later


def shards(queries, key_vectors, value_vectors, norm_gain, window_gain):
    tok_rows, model_width = queries.shape
    head_count = model_width // HEAD
    ctx_index = lax.axis_index("ctx")
    reach_blocks = WINDOW // tok_rows
    own_pair = (key_vectors, value_vectors)
    received = []
    travelling = own_pair
    for distance in range(reach_blocks):
        travelling = passed_along((travelling[0], travelling[1]), "ctx", 1)
        received.append(travelling)
    ordered = received[::-1] + [own_pair]
    window_keys = jnp.concatenate([member[0] for member in ordered], axis=0)
    window_values = jnp.concatenate([member[1] for member in ordered], axis=0)
    span_rows = window_keys.shape[0]
    query_place = ctx_index * tok_rows + jnp.arange(tok_rows, dtype=jnp.int32)
    key_place = (ctx_index - reach_blocks) * tok_rows + jnp.arange(span_rows, dtype=jnp.int32)
    inside = (
        (key_place[None, :] <= query_place[:, None])
        & (query_place[:, None] - key_place[None, :] < WINDOW)
        & (key_place[None, :] >= 0)
    )
    group_size = 4
    groups = head_count // group_size
    scale = 1.0 / math.sqrt(HEAD)

    def split_groups(matrix):
        return jnp.moveaxis(matrix.reshape(matrix.shape[0], groups, group_size, HEAD), 1, 0)

    def attend(operands):
        query_group, key_group, value_group = operands
        scores = (
            jnp.einsum("tge,sge->gts", query_group, key_group, preferred_element_type=jnp.float32)
            * scale
        )
        scores = jnp.where(inside[None], scores, -jnp.inf)
        peak = jnp.max(scores, axis=-1, keepdims=True)
        expos = jnp.exp(scores - peak)
        weights = (expos / jnp.sum(expos, axis=-1, keepdims=True)).astype(jnp.bfloat16)
        return jnp.einsum("gts,sge->tge", weights, value_group, preferred_element_type=jnp.float32)

    attended = lax.map(
        attend, (split_groups(queries), split_groups(window_keys), split_groups(window_values))
    )
    attended = jnp.moveaxis(attended, 0, 1).reshape(tok_rows, head_count, HEAD)
    windowed = attended * lax.rsqrt(jnp.mean(attended * attended, axis=-1, keepdims=True) + EPS)
    windowed = windowed * window_gain.reshape(head_count, HEAD)
    phi_query = feature_map(queries).reshape(tok_rows, head_count, HEAD)
    phi_key = feature_map(key_vectors).reshape(tok_rows, head_count, HEAD)
    value_heads = value_vectors.reshape(tok_rows, head_count, HEAD)
    local_state = jnp.einsum(
        "the,thf->hef", phi_key, value_heads, preferred_element_type=jnp.float32
    )
    carried = entering(local_state, "ctx", add_states, jnp.zeros_like(local_state))
    from_state = jnp.einsum(
        "the,hef->thf", phi_query, carried.astype(jnp.bfloat16), preferred_element_type=jnp.float32
    )
    affinity = jnp.einsum("the,she->hts", phi_query, phi_key, preferred_element_type=jnp.float32)
    inner = jnp.arange(tok_rows, dtype=jnp.int32)
    causal = inner[:, None] >= inner[None, :]
    affinity = jnp.where(causal[None], affinity, 0.0).astype(jnp.bfloat16)
    local_part = jnp.einsum(
        "hts,shf->thf", affinity, value_heads, preferred_element_type=jnp.float32
    )
    linear = from_state + local_part
    normed = linear * lax.rsqrt(jnp.mean(linear * linear, axis=-1, keepdims=True) + EPS)
    normed = normed * norm_gain.reshape(head_count, HEAD)
    return (windowed + normed).reshape(tok_rows, model_width).astype(jnp.bfloat16)


QA, QB, KK, VV, OA, OB, ST, SN = range(8)
EXP_SCALE = math.log2(math.e) / math.sqrt(HEAD)
LOW = -1e30


def nt(a, b):
    return lax.dot_general(a, b, (((1,), (1,)), ((), ())), preferred_element_type=jnp.float32)


def tn(a, b):
    return lax.dot_general(a, b, (((0,), (0,)), ((), ())), preferred_element_type=jnp.float32)


def tt(a, b):
    return lax.dot_general(a, b, (((0,), (1,)), ((), ())), preferred_element_type=jnp.float32)


def hub_kernel(
    n,
    q_ref, k_ref, v_ref, gn_ref, gw_ref, out_ref,
    qa, qb, kr, vr, oa_s, ob_s, st_s, sn_s, oa_r, ob_r, st_r, sn_r,
    q_own, k_own, v_own, send, recv, loaded,
):
    tok, width = q_ref.shape
    heads = width // HEAD
    me = lax.axis_index("ctx")
    left, right = me - 1, me + 1
    first, hub, last = 0, 1, n - 1

    def cols(h):
        return pl.ds(pl.multiple_of(h * HEAD, HEAD), HEAD)

    def move(stream, src, dst, h, target):
        return pltpu.make_async_remote_copy(
            src_ref=src,
            dst_ref=dst,
            send_sem=send.at[stream, h],
            recv_sem=recv.at[stream, h],
            device_id={"ctx": target},
            device_id_type=pl.DeviceIdType.MESH,
        )

    def q_left(h):
        return move(QA, q_ref.at[:, cols(h)], qa.at[:, cols(h)], h, left)

    def q_relay(h):
        return move(QB, qa.at[:, cols(h)], qb.at[:, cols(h)], h, left)

    def k_right(h):
        return move(KK, k_ref.at[:, cols(h)], kr.at[:, cols(h)], h, right)

    def v_right(h):
        return move(VV, v_ref.at[:, cols(h)], vr.at[:, cols(h)], h, right)

    def oa_right(h):
        return move(OA, oa_s.at[h], oa_r.at[h], h, right)

    def ob_right(h):
        return move(OB, ob_s.at[h], ob_r.at[h], h, right)

    def st_right(h):
        return move(ST, st_s.at[h], st_r.at[h], h, right)

    def sn_right(h):
        return move(SN, sn_s.at[h], sn_r.at[h], h, right)

    def each_head(body):
        def step(h, carry):
            body(h)
            return carry

        lax.fori_loop(0, heads, step, 0)

    loads = [
        pltpu.make_async_copy(src, dst, loaded.at[i])
        for i, (src, dst) in enumerate([(k_ref, k_own), (v_ref, v_own), (q_ref, q_own)])
    ]
    for load in loads:
        load.start()

    barrier = pltpu.get_barrier_semaphore()

    @pl.when(me > first)
    def _():
        pl.semaphore_signal(
            barrier, inc=1, device_id={"ctx": left}, device_id_type=pl.DeviceIdType.MESH
        )

    @pl.when(me < last)
    def _():
        pl.semaphore_signal(
            barrier, inc=1, device_id={"ctx": right}, device_id_type=pl.DeviceIdType.MESH
        )

    peers = (me > first).astype(jnp.int32) + (me < last).astype(jnp.int32)
    pl.semaphore_wait(barrier, peers)

    key_at = lax.broadcasted_iota(jnp.int32, (tok, tok), 0)
    query_at = lax.broadcasted_iota(jnp.int32, (tok, tok), 1)
    causal = key_at <= query_at

    def soft(scores, values):
        peak = functools.reduce(
            jnp.maximum, [jnp.max(s, axis=0, keepdims=True) for s in scores]
        )
        total, out = 0.0, 0.0
        for s, v in zip(scores, values):
            e = jnp.exp2((s - peak) * EXP_SCALE)
            total = total + jnp.sum(e, axis=0, keepdims=True)
            out = out + tn(v, e.astype(jnp.bfloat16))
        return peak, total, out

    def normalised(soft_sum):
        peak, total, out = soft_sum
        return peak + jnp.log2(total) * (1.0 / EXP_SCALE), out * (1.0 / total)

    def merge(one, level, out):
        top = jnp.maximum(one[0], level)
        f1 = jnp.exp2((one[0] - top) * EXP_SCALE)
        f2 = jnp.exp2((level - top) * EXP_SCALE)
        return top, one[1] * f1 + f2, one[2] * f1 + out.astype(jnp.float32) * f2

    def local_linear(q, phi_k, v):
        phi_q = feature_map(q)
        affinity = jnp.where(causal, nt(phi_k, phi_q), 0.0).astype(jnp.bfloat16)
        return phi_q, tn(v, affinity)

    def finish(h, soft_sum, linear):
        _, total, out = soft_sum
        att = out * (1.0 / total)
        att = att * lax.rsqrt(jnp.mean(att * att, axis=0, keepdims=True) + EPS)
        lin = linear * lax.rsqrt(jnp.mean(linear * linear, axis=0, keepdims=True) + EPS)
        row = att.T * gw_ref[pl.ds(h, 1), :] + lin.T * gn_ref[pl.ds(h, 1), :]
        out_ref[:, cols(h)] = row.astype(jnp.bfloat16)

    def diagonal(q, k):
        return jnp.where(causal, nt(k, q), LOW)

    @pl.when(me == first)
    def _():
        def start(h):
            k_right(h).start()
            v_right(h).start()

        each_head(start)

        for load in loads:
            load.wait()

        def compute(h):
            q, k, v = q_own[:, cols(h)], k_own[:, cols(h)], v_own[:, cols(h)]
            _, linear = local_linear(q, feature_map(k), v)
            finish(h, soft([diagonal(q, k)], [v]), linear)

        each_head(compute)

        def drain(h):
            k_right(h).wait_send()
            v_right(h).wait_send()

        each_head(drain)

    @pl.when(me == hub)
    def _():
        for load in loads:
            load.wait()

        def compute(h, later_first):
            q, k, v = q_own[:, cols(h)], k_own[:, cols(h)], v_own[:, cols(h)]
            phi_k = feature_map(k)
            state = tn(phi_k, v)
            k_right(h).wait_recv()
            v_right(h).wait_recv()
            k0, v0 = kr[:, cols(h)], vr[:, cols(h)]
            before = tn(feature_map(k0), v0)
            sn_s[h] = (before + state).astype(jnp.bfloat16)
            sn_right(h).start()

            def part(arrival, queries, row, target, sending):
                arrival(h).wait_recv()
                other = queries[:, cols(h)]
                level, out = normalised(soft([nt(k0, other), nt(k, other)], [v0, v]))
                target[h] = out.astype(jnp.bfloat16)
                st_s[h, row : row + 1] = level
                return sending(h)

            part_a = (q_left, qa, 0, oa_s, oa_right)
            part_b = (q_relay, qb, 1, ob_s, ob_right)
            order = (part_b, part_a) if later_first else (part_a, part_b)
            part(*order[0]).start()
            second = part(*order[1])
            st_right(h).start()
            second.start()
            phi_q, linear = local_linear(q, phi_k, v)
            linear = linear + tt(before.astype(jnp.bfloat16), phi_q)
            finish(h, soft([nt(k0, q), diagonal(q, k)], [v0, v]), linear)

        compute(0, False)

        def step(h, carry):
            compute(h, True)
            return carry

        lax.fori_loop(1, heads, step, 0)

        def drain(h):
            st_right(h).wait_send()
            ob_right(h).wait_send()
            sn_right(h).wait_send()
            oa_right(h).wait_send()

        each_head(drain)

    @pl.when((me > hub) & (me < last))
    def _():
        q_left(0).start()
        q_left(1).start()

        def relay(h):
            q_left(h).wait_recv()
            q_relay(h).start()

            @pl.when((h > 0) & (h < heads - 1))
            def _():
                q_left(h + 1).start()

        each_head(relay)

        for load in loads:
            load.wait()

        def compute(h):
            q, k, v = q_own[:, cols(h)], k_own[:, cols(h)], v_own[:, cols(h)]
            phi_k = feature_map(k)
            phi_q, linear = local_linear(q, phi_k, v)
            state = tn(phi_k, v)
            other = soft([nt(k, qa[:, cols(h)])], [v])
            own = soft([diagonal(q, k)], [v])
            sn_right(h).wait_recv()
            carried = sn_r[h]
            sn_s[h] = (carried.astype(jnp.float32) + state).astype(jnp.bfloat16)
            sn_right(h).start()
            linear = linear + tt(carried, phi_q)
            st_right(h).wait_recv()
            ob_right(h).wait_recv()
            level, out = normalised(merge(other, st_r[h, 1:2], ob_r[h]))
            oa_s[h] = out.astype(jnp.bfloat16)
            st_s[h, 0:1] = level
            st_s[h, 1:2] = level
            st_right(h).start()
            oa_right(h).start()
            oa_right(h).wait_recv()
            finish(h, merge(own, st_r[h, 0:1], oa_r[h]), linear)

        each_head(compute)

        def drain(h):
            q_left(h).wait_send()
            q_relay(h).wait_send()
            st_right(h).wait_send()
            oa_right(h).wait_send()
            sn_right(h).wait_send()

        each_head(drain)

    @pl.when(me == last)
    def _():
        def start(h):
            q_left(h).start()

        each_head(start)

        for load in loads:
            load.wait()

        def compute(h):
            q, k, v = q_own[:, cols(h)], k_own[:, cols(h)], v_own[:, cols(h)]
            phi_q, linear = local_linear(q, feature_map(k), v)
            own = soft([diagonal(q, k)], [v])
            sn_right(h).wait_recv()
            linear = linear + tt(sn_r[h], phi_q)
            st_right(h).wait_recv()
            oa_right(h).wait_recv()
            finish(h, merge(own, st_r[h, 0:1], oa_r[h]), linear)

        each_head(compute)

        def drain(h):
            q_left(h).wait_send()

        each_head(drain)


def hub_shards(n, queries, key_vectors, value_vectors, norm_gain, window_gain):
    tok, width = queries.shape
    heads = width // HEAD
    vmem = pl.BlockSpec(memory_space=pltpu.VMEM)
    hbm = pl.BlockSpec(memory_space=pl.ANY)
    block = pltpu.VMEM((tok, width), jnp.bfloat16)
    partial = pltpu.VMEM((heads, HEAD, tok), jnp.bfloat16)
    stats = pltpu.VMEM((heads, 2, tok), jnp.float32)
    state = pltpu.VMEM((heads, HEAD, HEAD), jnp.bfloat16)
    return pl.pallas_call(
        functools.partial(hub_kernel, n),
        out_shape=pltpu.VMEM((tok, width), jnp.bfloat16),
        in_specs=[hbm] * 3 + [vmem] * 2,
        out_specs=vmem,
        scratch_shapes=[block] * 4
        + [partial, partial, stats, state] * 2
        + [block] * 3
        + [pltpu.SemaphoreType.DMA((8, heads)), pltpu.SemaphoreType.DMA((8, heads))]
        + [pltpu.SemaphoreType.DMA((3,))],
        compiler_params=pltpu.CompilerParams(
            collective_id=0, has_side_effects=True, vmem_limit_bytes=56 * 2**20
        ),
        name="hub_attention",
    )(
        queries,
        key_vectors,
        value_vectors,
        norm_gain.reshape(heads, HEAD),
        window_gain.reshape(heads, HEAD),
    )


def solution(mesh):
    count = mesh.shape["ctx"]

    def run(queries, key_vectors, value_vectors, norm_gain, window_gain):
        args = (queries, key_vectors, value_vectors, norm_gain, window_gain)
        fits = count * queries.shape[0] <= WINDOW
        if fits and count - 2 == 2:
            return hub_shards(count, *args)
        return shards(*args)

    return jax.shard_map(
        run,
        mesh=mesh,
        in_specs=(P(("dp", "ctx"), None), P(("dp", "ctx"), None), P(("dp", "ctx"), None), P(), P()),
        out_specs=P(("dp", "ctx"), None),
        check_vma=False,
    )
```
